768 devices in a mesh: section: 8 (over x, y_lo), seq: 24 (over z, core), rep: 4 (over y_hi).
Axes of the slice: x: 4, y: 8 (y_hi: 4, y_lo: 2; y = y_hi * 2 + y_lo), z: 12, core: 2. Of those that a mesh axis runs over, the one named last changes fastest.
Arguments:
- char_queries: bfloat16 [4, 8, 6144, 2048], P('rep', 'section', 'seq'), may hold values from -34 to 34
- char_keys: bfloat16 [4, 8, 6144, 2048], P('rep', 'section', 'seq'), may hold values from -6 to 6
- char_values: bfloat16 [4, 8, 6144, 2048], P('rep', 'section', 'seq'), may hold values from -48 to 48
- doc_starts: int32 [4, 8, 48], P('rep', 'section'), may hold values from 0 to 6143, as said below
- key_weight: bfloat16 [8, 2048, 1024], P('section'), may hold values from -0.125 to 0.125
- norm_gain: float32 [8, 2048], P('section'), may hold values from 0.25 to 1.75
- stashed: bfloat16 [4, 8, 2, 1536, 2048], P('rep', 'section', None, 'seq'), may hold values from -48 to 48
- cotangent: bfloat16 [4, 8, 1536, 1024], P('rep', 'section', 'seq'), may hold values from -6 to 6
- plan_slot: int32 [4, 8], P('rep', 'section'), may hold values from 0 to 1
Outputs:
- mol_keys: bfloat16 [4, 8, 1536, 1024], P('rep', 'section', 'seq')
- upstream_grad: bfloat16 [4, 8, 1536, 2048], P('rep', 'section', 'seq')
- gain_update: float32 [8, 2048], P('section')
The draws below stay inside these ranges and needn't reach their ends.
Inputs may be any that keep to these rules, and one draw needn't show every extreme that they name: `doc_starts`: each row of offsets rises strictly, begins with 0 and ends with 6143.
All inputs are finite; a program needn't handle non-finite values.
Results may differ from the reference program's by a relative error of at most 0.012.
Values may be sent and summed in bfloat16 or wider, within the bound.
A program may use at most 64 MiB of HBM per device.

```python
import math
import jax
import jax.numpy as jnp
from jax import lax

HEADS = 32
HEAD_DIM = 64
D = 2048
KEY_WIDTH = 1024
POOL = 4
CH_DEV = 256
WINDOW = 128
SLOTS = 2
REPLICAS = 4
SECTIONS = 8
CHARS = 6144
MOL = 1536
DOCS = 48
N_SEQ = 24


def doc_offsets(key):
    row_keys = jax.random.split(jax.random.fold_in(key, 7), REPLICAS * SECTIONS)

    def one_row(row_key):
        chosen = jax.random.permutation(row_key, CHARS - 2)[:DOCS - 2] + 1
        return jnp.concatenate([jnp.zeros((1,), jnp.int32), jnp.sort(chosen).astype(jnp.int32), jnp.full((1,), CHARS - 1, jnp.int32)])
    return jax.vmap(one_row)(row_keys).reshape(REPLICAS, SECTIONS, DOCS)


def draw_doc_starts(key, part):
    return doc_offsets(key)


def draw_char_queries(key, part):
    gaussian = jnp.clip(jax.random.normal(jax.random.fold_in(key, 23), (REPLICAS, SECTIONS, CHARS, D)), -6.0, 6.0)
    return gaussian.astype(jnp.bfloat16)


def draw_char_keys(key, part):
    gaussian = jnp.clip(jax.random.normal(jax.random.fold_in(key, 19), (REPLICAS, SECTIONS, CHARS, D)), -6.0, 6.0)
    return gaussian.astype(jnp.bfloat16)


def scaled_noise(key, full_shape):
    column_shape = full_shape[:-2] + (1, full_shape[-1])
    row_shape = full_shape[:-1] + (1,)
    gaussian = jnp.clip(jax.random.normal(jax.random.fold_in(key, 29), full_shape), -4.0, 4.0)
    column_scale = jnp.exp(jax.random.uniform(jax.random.fold_in(key, 31), column_shape, jnp.float32, 0.0, math.log(10.0)))
    row_scale = jnp.exp(jax.random.uniform(jax.random.fold_in(key, 37), row_shape, jnp.float32, 0.0, math.log(4.0)))
    return 0.3 * gaussian * column_scale * row_scale


def draw_char_values(key, part):
    return scaled_noise(jax.random.fold_in(key, 41), (REPLICAS, SECTIONS, CHARS, D)).astype(jnp.bfloat16)


def draw_stashed(key, part):
    return scaled_noise(jax.random.fold_in(key, 43), (REPLICAS, SECTIONS, SLOTS, MOL, D)).astype(jnp.bfloat16)


def place_ends(result, stream_key, least, top_value):
    shape = result.shape
    spot = [jax.random.randint(jax.random.fold_in(stream_key, axis), (), 0, shape[axis]) for axis in range(len(shape))]
    result = result.at[tuple(spot)].set(least)
    longest = shape.index(max(shape))
    spot[longest] = (spot[longest] + 1) % shape[longest]
    return result.at[tuple(spot)].set(top_value)


def shard_levels(key, shape, cuts, least, top_value):
    factor_of = 1.0
    for position, shards_of in cuts:
        heights = jax.random.uniform(jax.random.fold_in(jax.random.fold_in(key, 6), position), (shards_of,), jnp.float32, least / len(cuts), top_value / len(cuts))
        factor_of = factor_of * jnp.repeat(jnp.exp(heights), shape[position] // shards_of).reshape((-1,) + (1,) * (len(shape) - 1 - position))
    return factor_of


def scatter_about(rng, extent, scale, bound, shards=(), kind=jnp.bfloat16):
    result = jax.random.normal(rng, extent, jnp.float32) * scale
    if len(shards) > 0:
        result = shard_levels(rng, extent, shards, -0.22, 0.18) * result
    return jnp.clip(result, min=-bound, max=bound).astype(kind)


def setup_inputs(seed: int = 0) -> dict:
    key_list = jax.random.split(jax.random.key(seed), 10)
    return {
        "char_queries": draw_char_queries(jax.random.fold_in(key_list[9], 71), 0),
        "char_keys": draw_char_keys(jax.random.fold_in(key_list[9], 71), 0),
        "char_values": draw_char_values(jax.random.fold_in(key_list[9], 71), 0),
        "doc_starts": draw_doc_starts(jax.random.fold_in(key_list[9], 71), 0),
        "key_weight": scatter_about(key_list[4], (SECTIONS, D, KEY_WIDTH), D ** -0.5, 0.125, ((0, 8),)),
        "norm_gain": jnp.clip(1.0 + 0.15 * jax.random.normal(key_list[5], (SECTIONS, D), jnp.float32), 0.25, 1.75),
        "stashed": draw_stashed(jax.random.fold_in(key_list[9], 71), 0),
        "cotangent": scatter_about(key_list[7], (REPLICAS, SECTIONS, MOL, KEY_WIDTH), 1.0, 6.0, ((0, 4), (1, 8), (2, 24))),
        "plan_slot": place_ends(jax.random.randint(key_list[8], (REPLICAS, SECTIONS), 0, SLOTS), jax.random.fold_in(key_list[8], 1), 0, SLOTS - 1).astype(jnp.int32),
    }


EPS_NORM = 1e-05
EPS_STEP = 1e-06

def doc_index(positions, offsets):
    return lax.optimization_barrier(jnp.sum((offsets[None, :] <= positions[:, None]).astype(jnp.int32), axis=1))

def attend(block_queries, block_keys, block_values, query_pos, key_pos, offsets):
    row_count = block_queries.shape[0]
    key_count = block_keys.shape[0]
    query_doc = doc_index(query_pos, offsets)
    key_doc = doc_index(key_pos, offsets)
    allowed = (key_doc[None, :] == query_doc[:, None]) & (key_pos[None, :] <= query_pos[:, None]) & (key_pos[None, :] > query_pos[:, None] - WINDOW)
    heads_query = block_queries.astype(jnp.float32).reshape(row_count, HEADS, HEAD_DIM)
    heads_key = block_keys.astype(jnp.float32).reshape(key_count, HEADS, HEAD_DIM)
    heads_value = block_values.astype(jnp.float32).reshape(key_count, HEADS, HEAD_DIM)
    scores = jnp.einsum('qhd,khd->hqk', heads_query, heads_key) * (1.0 / math.sqrt(HEAD_DIM))
    scores = jnp.where(allowed[None, :, :], scores, -1e+30)
    row_max = lax.optimization_barrier(jnp.max(scores, axis=2, keepdims=True))
    weights = jnp.exp(scores - row_max)
    row_total = lax.optimization_barrier(jnp.sum(weights, axis=2, keepdims=True))
    rounded = lax.optimization_barrier(weights.astype(jnp.bfloat16)).astype(jnp.float32)
    mixed_heads = jnp.einsum('hqk,khd->qhd', rounded, heads_value)
    return (mixed_heads / jnp.transpose(row_total, (1, 0, 2))).reshape(row_count, D).astype(jnp.bfloat16)

def character_row(row_queries, row_keys, row_values, offsets):
    padded_keys = jnp.concatenate([jnp.zeros((WINDOW, D), row_keys.dtype), row_keys], axis=0)
    padded_values = jnp.concatenate([jnp.zeros((WINDOW, D), row_values.dtype), row_values], axis=0)

    def block(block_index):
        block_start = block_index * CH_DEV
        block_queries = lax.dynamic_slice_in_dim(row_queries, block_start, CH_DEV, 0)
        block_keys = lax.dynamic_slice_in_dim(padded_keys, block_start, CH_DEV + WINDOW, 0)
        block_values = lax.dynamic_slice_in_dim(padded_values, block_start, CH_DEV + WINDOW, 0)
        query_pos = block_start + jnp.arange(CH_DEV, dtype=jnp.int32)
        key_pos = block_start - WINDOW + jnp.arange(CH_DEV + WINDOW, dtype=jnp.int32)
        return attend(block_queries, block_keys, block_values, query_pos, key_pos, offsets)
    blocks = lax.map(block, jnp.arange(N_SEQ, dtype=jnp.int32))
    return blocks.reshape(CHARS, D)

def reference(char_queries, char_keys, char_values, doc_starts, key_weight, norm_gain, stashed, cotangent, plan_slot):

    def one_row(row_index):
        rep_index = row_index // SECTIONS
        section_index = row_index % SECTIONS
        return character_row(char_queries[rep_index, section_index], char_keys[rep_index, section_index], char_values[rep_index, section_index], doc_starts[rep_index, section_index])
    attended = lax.map(one_row, jnp.arange(REPLICAS * SECTIONS, dtype=jnp.int32)).reshape(REPLICAS, SECTIONS, CHARS, D)
    pooled = lax.optimization_barrier(jnp.mean(attended.astype(jnp.float32).reshape(REPLICAS, SECTIONS, MOL, POOL, D), axis=3)).astype(jnp.bfloat16)
    arrived = jnp.roll(pooled, 1, axis=1)
    as_float = arrived.astype(jnp.float32)
    inv_norm = lax.rsqrt(lax.optimization_barrier(jnp.mean(as_float * as_float, axis=3, keepdims=True)) + EPS_NORM)
    normed = (as_float * inv_norm * norm_gain[None, :, None, :]).astype(jnp.bfloat16)
    mol_keys = jnp.einsum('rsmd,sdk->rsmk', normed.astype(jnp.float32), key_weight.astype(jnp.float32)).astype(jnp.bfloat16)
    chooser = jnp.arange(SLOTS, dtype=jnp.int32)[None, None, :] == plan_slot[:, :, None]
    held_rows = lax.optimization_barrier(jnp.sum(jnp.where(chooser[:, :, :, None, None], stashed.astype(jnp.float32), jnp.float32(0.0)), axis=2))
    back_grad = jnp.einsum('rsmk,sdk->rsmd', cotangent.astype(jnp.float32), key_weight.astype(jnp.float32))
    inv_rms = lax.rsqrt(lax.optimization_barrier(jnp.mean(held_rows * held_rows, axis=3, keepdims=True)) + EPS_NORM)
    whitened = held_rows * inv_rms
    gain_sum = lax.optimization_barrier(jnp.sum(back_grad * whitened, axis=(0, 2)))
    gain_update = gain_sum / jnp.sqrt(lax.optimization_barrier(jnp.mean(gain_sum * gain_sum, axis=1, keepdims=True)) + EPS_STEP)
    scaled = back_grad * norm_gain[None, :, None, :]
    dinput = (inv_rms * (scaled - whitened * lax.optimization_barrier(jnp.mean(scaled * whitened, axis=3, keepdims=True)))).astype(jnp.bfloat16)
    upstream_grad = jnp.roll(dinput, -1, axis=1)
    return (mol_keys, upstream_grad, gain_update)
```

```python
import functools
import math

import jax
import jax.numpy as jnp
from jax import lax
from jax.experimental import pallas as pl
from jax.experimental.pallas import tpu as pltpu
from jax.sharding import PartitionSpec as P

HEAD_DIM = 64
POOL = 4
WINDOW = 128
EPS_NORM = 1e-05
EPS_STEP = 1e-06
LOG2E = math.log2(math.e)
MESH = pl.DeviceIdType.MESH
F32 = jnp.float32
BF16 = jnp.bfloat16


def kernel(
    nsec,
    nseq,
    nrep,
    chunks,
    q_hbm,
    k_hbm,
    v_hbm,
    doc_ref,
    w_hbm,
    gain_ref,
    st_hbm,
    cot_hbm,
    slot_ref,
    mol_ref,
    up_ref,
    gu_ref,
    q_raw,
    q_buf,
    k_buf,
    v_buf,
    w_buf,
    st_buf,
    cot_buf,
    bias,
    bg_buf,
    din,
    pooled,
    arrived,
    acc,
    g_own,
    r1,
    r2,
    r3,
    loc_sem,
    kv_send,
    kv_recv,
    up_send,
    up_recv,
    po_send,
    po_recv,
    p1_send,
    p1_recv,
    p2_send,
    p2_recv,
    p3_send,
    p3_recv,
):
    rows, width = q_raw.shape
    half = rows // 2
    mol_rows, key_width = acc.shape
    mol_half = mol_rows // 2
    nz = nseq // 2
    nown = nrep * 2
    part = width // nown
    cw = width // chunks
    pairs = cw // 128

    sec = lax.axis_index("section")
    seq = lax.axis_index("seq")
    rep = lax.axis_index("rep")
    core = lax.rem(seq, 2)
    z = lax.div(seq, 2)
    me = rep * 2 + core
    sec_next = lax.rem(sec + 1, nsec)
    sec_prev = lax.rem(sec + nsec - 1, nsec)
    seq_next = lax.rem(seq + 1, nseq)
    seq_prev = lax.rem(seq + nseq - 1, nseq)
    across = lax.rem(seq + nseq + 2 * core - 1, nseq)

    def owner_id(d):
        other = lax.rem(me + d, nown)
        return other, {"seq": z * 2 + lax.rem(other, 2), "rep": lax.div(other, 2)}

    def z_id(d):
        other = lax.rem(z + d, nz)
        return other, {"seq": other * 2 + core}

    loads = {}

    def load(name, index, src, dst):
        loads[name] = pltpu.make_async_copy(src, dst, loc_sem.at[index])
        loads[name].start()

    load("cot", 0, cot_hbm.at[0, 0], cot_buf)
    load("st", 1, st_hbm.at[0, 0], st_buf)
    load("w", 2, w_hbm.at[0], w_buf)
    load("q", 3, q_hbm.at[0, 0], q_raw)
    load("k", 4, k_hbm.at[0, 0], k_buf.at[pl.ds(half, rows)])
    load("v", 5, v_hbm.at[0, 0], v_buf.at[pl.ds(half, rows)])

    barrier = pltpu.get_barrier_semaphore()
    peers = [{"seq": across}, {"section": sec_next}, {"section": sec_prev}]
    peers += [owner_id(d)[1] for d in range(1, nown)]
    peers += [z_id(d)[1] for d in range(1, nz)]
    for peer in peers:
        pl.semaphore_signal(barrier, inc=1, device_id=peer, device_id_type=MESH)
    pl.semaphore_wait(barrier, len(peers))

    def remote(src, dst, send, recv, to):
        return pltpu.make_async_remote_copy(
            src_ref=src, dst_ref=dst, send_sem=send, recv_sem=recv, device_id=to, device_id_type=MESH
        )

    halo = []
    for c in range(chunks):
        cols = pl.ds(c * cw, cw)
        for i, (src, dst) in enumerate(((k_hbm, k_buf), (v_hbm, v_buf))):
            copy = remote(
                src.at[0, 0, pl.ds(half, half), cols],
                dst.at[pl.ds(0, half), cols],
                kv_send.at[2 * c + i],
                kv_recv.at[2 * c + i],
                {"seq": seq_next},
            )
            copy.start()
            halo.append(copy)

    for name in ("cot", "st", "w"):
        loads[name].wait()
    slot = slot_ref[0, 0]
    square = jnp.zeros((mol_rows, 1), F32)
    for c in range(chunks):
        cols = pl.ds(c * cw, cw)
        held = st_buf[slot, :, cols].astype(F32)
        square += jnp.sum(held * held, axis=1, keepdims=True)
    inv_rms = lax.rsqrt(square / width + EPS_NORM)
    cot = cot_buf[...]
    mixed = jnp.zeros((mol_rows, 1), F32)
    for c in range(chunks):
        cols = pl.ds(c * cw, cw)
        back = lax.dot_general(cot, w_buf[cols, :], (((1,), (1,)), ((), ())), preferred_element_type=F32)
        whitened = st_buf[slot, :, cols].astype(F32) * inv_rms
        term = back * whitened
        scaled = back * gain_ref[:, cols]
        bg_buf[:, cols] = scaled
        mixed += jnp.sum(scaled * whitened, axis=1, keepdims=True)
        total = jnp.sum(term, axis=0, keepdims=True)
        for i in range(cw // part):
            g_own[c * (cw // part) + i] = total[:, i * part : (i + 1) * part]
    mixed = mixed / width
    for c in range(chunks):
        cols = pl.ds(c * cw, cw)
        whitened = st_buf[slot, :, cols].astype(F32) * inv_rms
        din[:, cols] = (inv_rms * (bg_buf[:, cols] - whitened * mixed)).astype(BF16)

    phase1 = []
    for d in range(1, nown):
        other, to = owner_id(d)
        copy = remote(g_own.at[other], r1.at[d], p1_send.at[d], p1_recv.at[d], to)
        copy.start()
        phase1.append(copy)
    up_copy = remote(din, up_ref.at[0, 0], up_send.at[0], up_recv.at[0], {"section": sec_prev})
    up_copy.start()

    loads["q"].wait()
    row = lax.broadcasted_iota(jnp.int32, (rows, rows), 0)
    col = lax.broadcasted_iota(jnp.int32, (rows, rows), 1)
    inner = lax.rem(row, half)
    source = (row - inner) + POOL * lax.rem(inner, mol_half) + lax.div(inner, mol_half)
    perm = jnp.where(col == source, F32(1.0 / math.sqrt(HEAD_DIM)), F32(0.0)).astype(BF16)
    lane = lax.rem(lax.broadcasted_iota(jnp.int32, (rows, 128), 1), 128)
    for c in range(chunks):
        moved = jnp.dot(perm, q_raw[:, pl.ds(c * cw, cw)], preferred_element_type=F32)
        for i in range(pairs):
            cols = pl.ds(c * cw + i * 128, 128)
            piece = moved[:, i * 128 : (i + 1) * 128]
            first = jnp.where(lane < HEAD_DIM, piece, 0.0).astype(BF16)
            second = jnp.where(lane < HEAD_DIM, 0.0, piece).astype(BF16)
            for b in range(2):
                q_buf[b, pl.ds(0, half), cols] = first[b * half : (b + 1) * half]
                q_buf[b, pl.ds(half, half), cols] = second[b * half : (b + 1) * half]

    offsets = doc_ref[0].astype(F32)
    q_row = lax.broadcasted_iota(jnp.int32, (half, 1), 0)
    q_in = POOL * lax.rem(q_row, mol_half) + lax.div(q_row, mol_half)
    k_in = lax.broadcasted_iota(jnp.int32, (half, 2 * half), 1)
    for b in range(2):
        start = seq * rows + b * half
        q_pos = (q_in + start).astype(F32)
        begin = jnp.max(jnp.where(offsets <= q_pos, offsets, -1.0), axis=1, keepdims=True)
        allowed = (
            (k_in > q_in + (half - WINDOW)) & (k_in <= q_in + half) & ((k_in + (start - half)).astype(F32) >= begin)
        )
        bias[b] = jnp.where(allowed, F32(0.0), F32(-1e30))

    lane_o = lax.broadcasted_iota(jnp.int32, (half, 128), 1)
    fours = jnp.full((2 * half, 128), POOL, BF16)

    def attend(b, first_pair, count):
        def one_pair(i, carry):
            cols = pl.ds(pl.multiple_of((first_pair + i) * 128, 128), 128)
            keys = k_buf[pl.ds(b * half, 2 * half), cols]
            values = v_buf[pl.ds(b * half, 2 * half), cols]
            scores = lax.dot_general(q_buf[b, :, cols], keys, (((1,), (1,)), ((), ())), preferred_element_type=F32)
            blocked = bias[b]
            weights = []
            for h in range(2):
                s = scores[h * half : (h + 1) * half] + blocked
                top = jnp.max(s, axis=1, keepdims=True)
                weights.append(jnp.exp2((s - top) * LOG2E).astype(BF16))
            mixed_heads = jnp.dot(
                jnp.concatenate(weights, axis=0),
                jnp.concatenate([values, fours], axis=1),
                preferred_element_type=F32,
            )
            low = lane_o < HEAD_DIM
            top_half, bottom_half = mixed_heads[:half], mixed_heads[half:]
            out = jnp.where(low, top_half[:, :128], bottom_half[:, :128]) / jnp.where(
                low, top_half[:, 128:], bottom_half[:, 128:]
            )
            mean = out[:mol_half]
            for t in range(1, POOL):
                mean += out[t * mol_half : (t + 1) * mol_half]
            pooled[pl.ds(b * mol_half, mol_half), cols] = mean.astype(BF16)
            return carry

        lax.fori_loop(0, count, one_pair, 0)

    relay = []

    def send_pooled(index, rows_at, cols):
        copy = remote(
            pooled.at[rows_at, cols],
            arrived.at[rows_at, cols],
            po_send.at[index],
            po_recv.at[index],
            {"section": sec_next},
        )
        copy.start()
        relay.append(copy)

    loads["k"].wait()
    loads["v"].wait()
    attend(1, 0, width // 128)
    send_pooled(chunks, pl.ds(mol_half, mol_half), pl.ds(0, width))

    for copy in phase1:
        copy.wait_recv()
    summed = g_own[me]
    for d in range(1, nown):
        summed += r1[d]
    r2[z] = summed
    phase2 = []
    for d in range(1, nz):
        other, to = z_id(d)
        copy = remote(r2.at[z], r2.at[z], p2_send.at[d], p2_recv.at[d], to)
        copy.start()
        phase2.append(copy)

    acc[...] = jnp.zeros_like(acc)
    square = jnp.zeros((mol_rows, 1), F32)
    phase3 = []

    def project(c, square):
        cols = pl.ds(c * cw, cw)
        relay[1 + c].wait_recv()
        got = arrived[:, cols].astype(F32)
        acc[...] += jnp.dot((got * gain_ref[:, cols]).astype(BF16), w_buf[cols, :], preferred_element_type=F32)
        return square + jnp.sum(got * got, axis=1, keepdims=True)

    for c in range(chunks):
        halo[2 * c].wait_recv()
        halo[2 * c + 1].wait_recv()
        attend(0, c * pairs, pairs)
        send_pooled(c, pl.ds(0, mol_half), pl.ds(c * cw, cw))
        if c == 0:
            relay[0].wait_recv()
        else:
            square = project(c - 1, square)
        if c == chunks - 2:
            for d in range(1, nz):
                other = lax.rem(z + nz - d, nz)
                remote(r2.at[z], r2.at[other], p2_send.at[d], p2_recv.at[d], {"seq": seq_next}).wait_recv()
            summed = r2[0]
            for i in range(1, nz):
                summed += r2[i]
            r3[me] = summed
            for d in range(1, nown):
                other, to = owner_id(d)
                copy = remote(r3.at[me], r3.at[me], p3_send.at[d], p3_recv.at[d], to)
                copy.start()
                phase3.append(copy)

    for d in range(1, nown):
        other = lax.rem(me + nown - d, nown)
        remote(r3.at[me], r3.at[other], p3_send.at[d], p3_recv.at[d], {"seq": seq_next}).wait_recv()
    power = jnp.zeros((1, 1), F32)
    for i in range(nown):
        power += jnp.sum(r3[i] * r3[i], axis=1, keepdims=True)
    inv_step = 1.0 / jnp.sqrt(power / width + EPS_STEP)
    for i in range(nown):
        gu_ref[:, pl.ds(i * part, part)] = r3[i] * inv_step

    for copy in halo:
        copy.wait_send()
    for copy in (*phase1, *phase2, *phase3):
        copy.wait_send()
    up_copy.wait()

    square = project(chunks - 1, square)
    mol_ref[0, 0] = (acc[...] * lax.rsqrt(square / width + EPS_NORM)).astype(BF16)
    for copy in relay:
        copy.wait_send()


def solution(mesh):
    nsec, nseq, nrep = (mesh.shape[a] for a in ("section", "seq", "rep"))

    def local(q, k, v, doc_starts, w, gain, stashed, cotangent, plan_slot):
        rows, width = q.shape[2:]
        key_width = w.shape[2]
        slots, mol_rows = stashed.shape[2:4]
        half = rows // 2
        chunks = 4 if width >= 2048 else 2
        nz, nown = nseq // 2, nrep * 2
        part = width // nown
        hbm = pl.BlockSpec(memory_space=pl.ANY)
        vmem = pl.BlockSpec(memory_space=pltpu.VMEM)
        smem = pl.BlockSpec(memory_space=pltpu.SMEM)
        dma = pltpu.SemaphoreType.DMA
        return pl.pallas_call(
            functools.partial(kernel, nsec, nseq, nrep, chunks),
            out_shape=(
                jax.ShapeDtypeStruct((1, 1, mol_rows, key_width), BF16),
                jax.ShapeDtypeStruct((1, 1, mol_rows, width), BF16),
                jax.ShapeDtypeStruct((1, width), F32),
            ),
            in_specs=[hbm, hbm, hbm, vmem, hbm, vmem, hbm, hbm, smem],
            out_specs=(vmem, hbm, vmem),
            scratch_shapes=[
                pltpu.VMEM((rows, width), BF16),
                pltpu.VMEM((2, rows, width), BF16),
                pltpu.VMEM((rows + half, width), BF16),
                pltpu.VMEM((rows + half, width), BF16),
                pltpu.VMEM((width, key_width), BF16),
                pltpu.VMEM((slots, mol_rows, width), BF16),
                pltpu.VMEM((mol_rows, key_width), BF16),
                pltpu.VMEM((2, half, 2 * half), F32),
                pltpu.VMEM((mol_rows, width), F32),
                pltpu.VMEM((mol_rows, width), BF16),
                pltpu.VMEM((mol_rows, width), BF16),
                pltpu.VMEM((mol_rows, width), BF16),
                pltpu.VMEM((mol_rows, key_width), F32),
                pltpu.VMEM((nown, 1, part), F32),
                pltpu.VMEM((nown, 1, part), F32),
                pltpu.VMEM((nz, 1, part), F32),
                pltpu.VMEM((nown, 1, part), F32),
                dma((6,)),
                dma((2 * chunks,)),
                dma((2 * chunks,)),
                dma((1,)),
                dma((1,)),
                dma((chunks + 1,)),
                dma((chunks + 1,)),
                dma((nown,)),
                dma((nown,)),
                dma((nz,)),
                dma((nz,)),
                dma((nown,)),
                dma((nown,)),
            ],
            compiler_params=pltpu.CompilerParams(
                collective_id=0, has_side_effects=True, vmem_limit_bytes=56 * 1024 * 1024
            ),
        )(q, k, v, doc_starts, w, gain, stashed, cotangent, plan_slot)

    in_specs = (
        P("rep", "section", "seq", None),
        P("rep", "section", "seq", None),
        P("rep", "section", "seq", None),
        P("rep", "section", None),
        P("section", None, None),
        P("section", None),
        P("rep", "section", None, "seq", None),
        P("rep", "section", "seq", None),
        P("rep", "section"),
    )
    out_specs = (
        P("rep", "section", "seq", None),
        P("rep", "section", "seq", None),
        P("section", None),
    )
    return jax.shard_map(local, mesh=mesh, in_specs=in_specs, out_specs=out_specs, check_vma=False)
```

```python
import functools
import math

import jax
import jax.numpy as jnp
from jax import lax
from jax.experimental import pallas as pl
from jax.experimental.pallas import tpu as pltpu
from jax.sharding import PartitionSpec as P

HEAD_DIM = 64
POOL = 4
WINDOW = 128
EPS_NORM = 1e-05
EPS_STEP = 1e-06
LOG2E = math.log2(math.e)
MESH = pl.DeviceIdType.MESH
F32 = jnp.float32
BF16 = jnp.bfloat16
IN_SPACE = pltpu.HBM
OUT_SHAPE = pltpu.VMEM


def kernel(
    nsec,
    nseq,
    nrep,
    chunks,
    q_hbm,
    k_hbm,
    v_hbm,
    doc_hbm,
    w_hbm,
    gain_hbm,
    st_hbm,
    cot_hbm,
    slot_hbm,
    mol_ref,
    up_ref,
    gu_ref,
    q_raw,
    q_buf,
    k_buf,
    v_buf,
    w_buf,
    st_buf,
    cot_buf,
    doc_ref,
    gain_ref,
    slot_ref,
    bias,
    bg_buf,
    din,
    pooled,
    arrived,
    acc,
    g_own,
    r1,
    r2,
    r3,
    loc_sem,
    ready,
    kv_send,
    kv_recv,
    up_send,
    up_recv,
    po_send,
    po_recv,
    p1_send,
    p1_recv,
    p2_send,
    p2_recv,
    p3_send,
    p3_recv,
):
    rows, width = q_raw.shape
    half = rows // 2
    mol_rows, key_width = acc.shape
    mol_half = mol_rows // 2
    nz = nseq // 2
    nown = nrep * 2
    part = width // nown
    cw = width // chunks
    pairs = cw // 128

    sec = lax.axis_index("section")
    seq = lax.axis_index("seq")
    rep = lax.axis_index("rep")
    core = lax.rem(seq, 2)
    z = lax.div(seq, 2)
    me = rep * 2 + core
    sec_next = lax.rem(sec + 1, nsec)
    sec_prev = lax.rem(sec + nsec - 1, nsec)
    seq_next = lax.rem(seq + 1, nseq)
    across = lax.rem(seq + nseq + 2 * core - 1, nseq)

    def owner_id(d):
        other = lax.rem(me + d, nown)
        return other, {"seq": z * 2 + lax.rem(other, 2), "rep": lax.div(other, 2)}

    def z_id(d):
        other = lax.rem(z + d, nz)
        return other, {"seq": other * 2 + core}

    def signal(sem, peers):
        for peer in peers:
            pl.semaphore_signal(sem, inc=1, device_id=peer, device_id_type=MESH)

    near_z = sorted({d % nz for d in (1, 2, -1, -2)} - {0})
    step_z = sorted({2 % nz, -2 % nz} - {0})
    near = [{"seq": across}, {"section": sec_next}, {"section": sec_prev}]
    near += [owner_id(d)[1] for d in range(1, nown)]
    near += [z_id(d)[1] for d in near_z]
    barrier = pltpu.get_barrier_semaphore()
    signal(barrier, near)

    loads = {}

    def load(name, src, dst):
        loads[name] = pltpu.make_async_copy(src, dst, loc_sem.at[len(loads)])
        loads[name].start()

    load("slot", slot_hbm, slot_ref)
    load("st", st_hbm.at[0, 0], st_buf)
    load("cot", cot_hbm.at[0, 0], cot_buf)
    load("gain", gain_hbm, gain_ref)
    for c in range(chunks):
        load("w%d" % c, w_hbm.at[0, pl.ds(c * cw, cw)], w_buf.at[pl.ds(c * cw, cw)])
    load("doc", doc_hbm.at[0], doc_ref)

    pl.semaphore_wait(barrier, len(near))
    signal(ready.at[0], [z_id(d)[1] for d in step_z])

    def remote(src, dst, send, recv, to):
        return pltpu.make_async_remote_copy(
            src_ref=src, dst_ref=dst, send_sem=send, recv_sem=recv, device_id=to, device_id_type=MESH
        )

    halo = []

    def send_halo(c):
        cols = pl.ds(c * cw, cw)
        for i, (src, dst) in enumerate(((k_hbm, k_buf), (v_hbm, v_buf))):
            copy = remote(
                src.at[0, 0, pl.ds(half, half), cols],
                dst.at[pl.ds(0, half), cols],
                kv_send.at[2 * c + i],
                kv_recv.at[2 * c + i],
                {"seq": seq_next},
            )
            copy.start()
            halo.append(copy)

    for c in range(chunks // 2):
        send_halo(c)

    for name in ("slot", "st"):
        loads[name].wait()
    slot = slot_ref[0, 0]
    square = jnp.zeros((mol_rows, 1), F32)
    for c in range(chunks):
        cols = pl.ds(c * cw, cw)
        held = st_buf[slot, :, cols].astype(F32)
        square += jnp.sum(held * held, axis=1, keepdims=True)
    inv_rms = lax.rsqrt(square / width + EPS_NORM)
    for name in ("cot", "gain"):
        loads[name].wait()
    cot = cot_buf[...]
    mixed = jnp.zeros((mol_rows, 1), F32)
    for c in range(chunks):
        cols = pl.ds(c * cw, cw)
        loads["w%d" % c].wait()
        back = lax.dot_general(cot, w_buf[cols, :], (((1,), (1,)), ((), ())), preferred_element_type=F32)
        whitened = st_buf[slot, :, cols].astype(F32) * inv_rms
        total = jnp.sum(back * whitened, axis=0, keepdims=True)
        for i in range(cw // part):
            g_own[c * (cw // part) + i] = total[:, i * part : (i + 1) * part]
        scaled = back * gain_ref[:, cols]
        bg_buf[:, cols] = scaled
        mixed += jnp.sum(scaled * whitened, axis=1, keepdims=True)

    phase1 = []
    for d in range(1, nown):
        other, to = owner_id(d)
        copy = remote(g_own.at[other], r1.at[d], p1_send.at[d], p1_recv.at[d], to)
        copy.start()
        phase1.append(copy)
    load("q", q_hbm.at[0, 0], q_raw)
    load("k", k_hbm.at[0, 0], k_buf.at[pl.ds(half, rows)])
    load("v", v_hbm.at[0, 0], v_buf.at[pl.ds(half, rows)])

    mixed = mixed / width
    for c in range(chunks):
        cols = pl.ds(c * cw, cw)
        whitened = st_buf[slot, :, cols].astype(F32) * inv_rms
        din[:, cols] = (inv_rms * (bg_buf[:, cols] - whitened * mixed)).astype(BF16)
    if step_z:
        pl.semaphore_wait(ready.at[0], len(step_z))
        signal(ready.at[1], [z_id(d)[1] for d in step_z])
    up_copy = remote(din, up_ref.at[0, 0], up_send.at[0], up_recv.at[0], {"section": sec_prev})
    up_copy.start()

    loads["doc"].wait()
    offsets = doc_ref[...].astype(F32)
    q_row = lax.broadcasted_iota(jnp.int32, (half, 1), 0)
    q_in = POOL * lax.rem(q_row, mol_half) + lax.div(q_row, mol_half)
    k_in = lax.broadcasted_iota(jnp.int32, (half, 2 * half), 1)
    for b in range(2):
        start = seq * rows + b * half
        q_pos = (q_in + start).astype(F32)
        begin = jnp.max(jnp.where(offsets <= q_pos, offsets, -1.0), axis=1, keepdims=True)
        allowed = (
            (k_in > q_in + (half - WINDOW)) & (k_in <= q_in + half) & ((k_in + (start - half)).astype(F32) >= begin)
        )
        bias[b] = jnp.where(allowed, F32(0.0), F32(-1e30))

    row = lax.broadcasted_iota(jnp.int32, (rows, rows), 0)
    col = lax.broadcasted_iota(jnp.int32, (rows, rows), 1)
    inner = lax.rem(row, half)
    source = (row - inner) + POOL * lax.rem(inner, mol_half) + lax.div(inner, mol_half)
    perm = jnp.where(col == source, F32(1.0 / math.sqrt(HEAD_DIM)), F32(0.0)).astype(BF16)
    lane = lax.broadcasted_iota(jnp.int32, (rows, 128), 1)
    loads["q"].wait()
    for c in range(chunks):
        moved = jnp.dot(perm, q_raw[:, pl.ds(c * cw, cw)], preferred_element_type=F32)
        for i in range(pairs):
            cols = pl.ds(c * cw + i * 128, 128)
            piece = moved[:, i * 128 : (i + 1) * 128]
            first = jnp.where(lane < HEAD_DIM, piece, 0.0).astype(BF16)
            second = jnp.where(lane < HEAD_DIM, 0.0, piece).astype(BF16)
            for b in range(2):
                q_buf[b, pl.ds(0, half), cols] = first[b * half : (b + 1) * half]
                q_buf[b, pl.ds(half, half), cols] = second[b * half : (b + 1) * half]

    low = lax.broadcasted_iota(jnp.int32, (half, 128), 1) < HEAD_DIM
    fours = jnp.full((2 * half, 128), POOL, BF16)

    def one_pair(b, pair):
        cols = pl.ds(pl.multiple_of(pair * 128, 128), 128)
        keys = k_buf[pl.ds(b * half, 2 * half), cols]
        values = v_buf[pl.ds(b * half, 2 * half), cols]
        scores = lax.dot_general(q_buf[b, :, cols], keys, (((1,), (1,)), ((), ())), preferred_element_type=F32)
        blocked = bias[b]
        weights = []
        for h in range(2):
            s = scores[h * half : (h + 1) * half] + blocked
            top = jnp.max(s, axis=1, keepdims=True)
            weights.append(jnp.exp2((s - top) * LOG2E).astype(BF16))
        mixed_heads = jnp.dot(
            jnp.concatenate(weights, axis=0),
            jnp.concatenate([values, fours], axis=1),
            preferred_element_type=F32,
        )
        first, second = mixed_heads[:half], mixed_heads[half:]
        out = jnp.where(low, first[:, :128], second[:, :128]) / jnp.where(low, first[:, 128:], second[:, 128:])
        mean = out[:mol_half]
        for t in range(1, POOL):
            mean += out[t * mol_half : (t + 1) * mol_half]
        pooled[pl.ds(b * mol_half, mol_half), cols] = mean.astype(BF16)

    def attend(b, first_pair, count):
        def two_pairs(i, carry):
            one_pair(b, first_pair + 2 * i)
            one_pair(b, first_pair + 2 * i + 1)
            return carry

        lax.fori_loop(0, count // 2, two_pairs, 0)

    relay = []

    def send_pooled(rows_at, cols):
        copy = remote(
            pooled.at[rows_at, cols],
            arrived.at[rows_at, cols],
            po_send.at[len(relay)],
            po_recv.at[len(relay)],
            {"section": sec_next},
        )
        copy.start()
        relay.append(copy)

    all_pairs = width // 128
    loads["k"].wait()
    loads["v"].wait()
    attend(1, 0, all_pairs // 2)

    for copy in phase1:
        copy.wait_recv()
    summed = g_own[me]
    for d in range(1, nown):
        summed += r1[d]
    r2[z] = summed
    if step_z:
        pl.semaphore_wait(ready.at[1], len(step_z))
    phase2 = []
    for d in range(1, nz):
        other, to = z_id(d)
        copy = remote(r2.at[z], r2.at[z], p2_send.at[d], p2_recv.at[d], to)
        copy.start()
        phase2.append(copy)
    for c in range(chunks // 2, chunks):
        send_halo(c)

    attend(1, all_pairs // 2, all_pairs // 2)
    send_pooled(pl.ds(mol_half, mol_half), pl.ds(0, width))
    acc[...] = jnp.zeros_like(acc)
    square = jnp.zeros((mol_rows, 1), F32)

    def near_part(c):
        halo[2 * c].wait_recv()
        halo[2 * c + 1].wait_recv()
        attend(0, c * pairs, pairs)
        send_pooled(pl.ds(0, mol_half), pl.ds(c * cw, cw))

    def project(c, square):
        cols = pl.ds(c * cw, cw)
        relay[1 + c].wait_recv()
        got = arrived[:, cols].astype(F32)
        acc[...] += jnp.dot((got * gain_ref[:, cols]).astype(BF16), w_buf[cols, :], preferred_element_type=F32)
        return square + jnp.sum(got * got, axis=1, keepdims=True)

    for c in range(chunks // 2):
        near_part(c)

    for d in range(1, nz):
        other = lax.rem(z + nz - d, nz)
        remote(r2.at[z], r2.at[other], p2_send.at[d], p2_recv.at[d], {"seq": seq_next}).wait_recv()
    summed = r2[0]
    for i in range(1, nz):
        summed += r2[i]
    r3[me] = summed
    phase3 = []
    for d in range(1, nown):
        other, to = owner_id(d)
        copy = remote(r3.at[me], r3.at[me], p3_send.at[d], p3_recv.at[d], to)
        copy.start()
        phase3.append(copy)

    relay[0].wait_recv()
    for c in range(chunks // 2, chunks):
        near_part(c)
        square = project(c - chunks // 2, square)
    for c in range(chunks - chunks // 2, chunks - 1):
        square = project(c, square)

    for d in range(1, nown):
        other = lax.rem(me + nown - d, nown)
        remote(r3.at[me], r3.at[other], p3_send.at[d], p3_recv.at[d], {"seq": seq_next}).wait_recv()
    power = jnp.zeros((1, 1), F32)
    for i in range(nown):
        power += jnp.sum(r3[i] * r3[i], axis=1, keepdims=True)
    inv_step = 1.0 / jnp.sqrt(power / width + EPS_STEP)
    for i in range(nown):
        gu_ref[:, pl.ds(i * part, part)] = r3[i] * inv_step

    square = project(chunks - 1, square)
    mol_ref[0, 0] = (acc[...] * lax.rsqrt(square / width + EPS_NORM)).astype(BF16)
    for copy in (*halo, *phase1, *phase2, *phase3, *relay):
        copy.wait_send()
    up_copy.wait()


def write_out(*refs):
    count = (len(refs) - 1) // 2
    sem = refs[-1]
    copies = [pltpu.make_async_copy(refs[i], refs[count + i], sem.at[i]) for i in range(count)]
    for copy in copies:
        copy.start()
    for copy in copies:
        copy.wait()


def solution(mesh):
    nsec, nseq, nrep = (mesh.shape[a] for a in ("section", "seq", "rep"))

    def local(q, k, v, doc_starts, w, gain, stashed, cotangent, plan_slot):
        rows, width = q.shape[2:]
        key_width = w.shape[2]
        slots, mol_rows = stashed.shape[2:4]
        half = rows // 2
        chunks = 4 if width >= 2048 else 2
        nz, nown = nseq // 2, nrep * 2
        part = width // nown
        hbm = pl.BlockSpec(memory_space=IN_SPACE)
        vmem = pl.BlockSpec(memory_space=pltpu.VMEM)
        dma = pltpu.SemaphoreType.DMA
        shapes = (
            ((1, 1, mol_rows, key_width), BF16),
            ((1, 1, mol_rows, width), BF16),
            ((1, width), F32),
        )
        results = pl.pallas_call(
            functools.partial(kernel, nsec, nseq, nrep, chunks),
            out_shape=tuple(OUT_SHAPE(s, t) for s, t in shapes),
            in_specs=[hbm] * 9,
            out_specs=(vmem, vmem, vmem),
            scratch_shapes=[
                pltpu.VMEM((rows, width), BF16),
                pltpu.VMEM((2, rows, width), BF16),
                pltpu.VMEM((rows + half, width), BF16),
                pltpu.VMEM((rows + half, width), BF16),
                pltpu.VMEM((width, key_width), BF16),
                pltpu.VMEM((slots, mol_rows, width), BF16),
                pltpu.VMEM((mol_rows, key_width), BF16),
                pltpu.VMEM((1, doc_starts.shape[2]), jnp.int32),
                pltpu.VMEM((1, width), F32),
                pltpu.SMEM((1, 1), jnp.int32),
                pltpu.VMEM((2, half, 2 * half), F32),
                pltpu.VMEM((mol_rows, width), F32),
                pltpu.VMEM((mol_rows, width), BF16),
                pltpu.VMEM((mol_rows, width), BF16),
                pltpu.VMEM((mol_rows, width), BF16),
                pltpu.VMEM((mol_rows, key_width), F32),
                pltpu.VMEM((nown, 1, part), F32),
                pltpu.VMEM((nown, 1, part), F32),
                pltpu.VMEM((nz, 1, part), F32),
                pltpu.VMEM((nown, 1, part), F32),
                dma((8 + chunks,)),
                pltpu.SemaphoreType.REGULAR((2,)),
                dma((2 * chunks,)),
                dma((2 * chunks,)),
                dma((1,)),
                dma((1,)),
                dma((chunks + 1,)),
                dma((chunks + 1,)),
                dma((nown,)),
                dma((nown,)),
                dma((nz,)),
                dma((nz,)),
                dma((nown,)),
                dma((nown,)),
            ],
            compiler_params=pltpu.CompilerParams(
                collective_id=0, has_side_effects=True, vmem_limit_bytes=56 * 1024 * 1024
            ),
        )(q, k, v, doc_starts, w, gain, stashed, cotangent, plan_slot)
        any_space = pl.BlockSpec(memory_space=pl.ANY)
        return pl.pallas_call(
            write_out,
            out_shape=tuple(jax.ShapeDtypeStruct(s, t) for s, t in shapes),
            in_specs=[vmem] * 3,
            out_specs=(any_space,) * 3,
            scratch_shapes=[dma((3,))],
        )(*(pltpu.with_memory_space_constraint(r, pltpu.VMEM) for r in results))

    in_specs = (
        P("rep", "section", "seq", None),
        P("rep", "section", "seq", None),
        P("rep", "section", "seq", None),
        P("rep", "section", None),
        P("section", None, None),
        P("section", None),
        P("rep", "section", None, "seq", None),
        P("rep", "section", "seq", None),
        P("rep", "section"),
    )
    out_specs = (
        P("rep", "section", "seq", None),
        P("rep", "section", "seq", None),
        P("section", None),
    )
    return jax.shard_map(local, mesh=mesh, in_specs=in_specs, out_specs=out_specs, check_vma=False)
```

```python
import functools
import math

import jax
import jax.numpy as jnp
from jax import lax
from jax.experimental import pallas as pl
from jax.experimental.pallas import tpu as pltpu
from jax.sharding import PartitionSpec as P

HEAD_DIM = 64
POOL = 4
WINDOW = 128
EPS_NORM = 1e-05
EPS_STEP = 1e-06
EARLY = 3
BEFORE = 3
CHUNKS = 4
UNROLL = 4
LOG2E = math.log2(math.e)
MESH = pl.DeviceIdType.MESH
F32 = jnp.float32
BF16 = jnp.bfloat16
IN_SPACE = pltpu.HBM
OUT_SHAPE = pltpu.VMEM


def kernel(
    nsec,
    nseq,
    nrep,
    chunks,
    q_hbm,
    k_hbm,
    v_hbm,
    doc_hbm,
    w_hbm,
    gain_hbm,
    st_hbm,
    cot_hbm,
    slot_hbm,
    mol_ref,
    up_ref,
    gu_ref,
    q_raw,
    q_buf,
    k_buf,
    v_buf,
    w_buf,
    st_buf,
    cot_buf,
    doc_ref,
    gain_ref,
    slot_ref,
    bias,
    bg_buf,
    din,
    pooled,
    arrived,
    acc,
    perm,
    g_own,
    r1,
    r2,
    r3,
    loc_sem,
    ready,
    kv_send,
    kv_recv,
    up_send,
    up_recv,
    po_send,
    po_recv,
    p1_send,
    p1_recv,
    p2_send,
    p2_recv,
    p3_send,
    p3_recv,
):
    rows, width = q_raw.shape
    half = rows // 2
    mol_rows, key_width = acc.shape
    mol_half = mol_rows // 2
    nz = nseq // 2
    nown = nrep * 2
    part = width // nown
    cw = width // chunks
    pairs = cw // 128

    sec = lax.axis_index("section")
    seq = lax.axis_index("seq")
    rep = lax.axis_index("rep")
    core = lax.rem(seq, 2)
    z = lax.div(seq, 2)
    me = rep * 2 + core
    sec_next = lax.rem(sec + 1, nsec)
    sec_prev = lax.rem(sec + nsec - 1, nsec)
    seq_next = lax.rem(seq + 1, nseq)
    across = lax.rem(seq + nseq + 2 * core - 1, nseq)

    def owner_id(d):
        other = lax.rem(me + d, nown)
        return other, {"seq": z * 2 + lax.rem(other, 2), "rep": lax.div(other, 2)}

    def z_id(d):
        other = lax.rem(z + d, nz)
        return other, {"seq": other * 2 + core}

    def signal(sem, peers):
        for peer in peers:
            pl.semaphore_signal(sem, inc=1, device_id=peer, device_id_type=MESH)

    near_z = sorted({d % nz for d in (1, 2, -1, -2)} - {0})
    step_z = sorted({2 % nz, -2 % nz} - {0})
    near = [{"seq": across}, {"section": sec_next}, {"section": sec_prev}]
    step_rep = sorted({1 % nrep, -1 % nrep} - {0})
    for d in [0] + step_rep:
        for e in range(2):
            if d or e:
                near.append({"seq": z * 2 + lax.rem(core + e, 2), "rep": lax.rem(rep + d, nrep)})
    near += [z_id(d)[1] for d in near_z]
    barrier = pltpu.get_barrier_semaphore()
    signal(barrier, near)

    loads = {}

    def load(name, src, dst):
        loads[name] = pltpu.make_async_copy(src, dst, loc_sem.at[len(loads)])
        loads[name].start()

    load("doc", doc_hbm.at[0], doc_ref)
    load("slot", slot_hbm, slot_ref)
    load("st", st_hbm.at[0, 0], st_buf)
    load("cot", cot_hbm.at[0, 0], cot_buf)
    load("gain", gain_hbm, gain_ref)
    for c in range(chunks):
        load("w%d" % c, w_hbm.at[0, pl.ds(c * cw, cw)], w_buf.at[pl.ds(c * cw, cw)])

    loads["doc"].wait()
    offsets = doc_ref[...].astype(F32)
    q_row = lax.broadcasted_iota(jnp.int32, (half, 1), 0)
    shift = mol_half.bit_length() - 1
    q_in = POOL * (q_row & (mol_half - 1)) + (q_row >> shift)
    k_in = lax.broadcasted_iota(jnp.int32, (half, 2 * half), 1)
    for b in range(2):
        start = seq * rows + b * half
        q_pos = (q_in + start).astype(F32)
        begin = jnp.max(jnp.where(offsets <= q_pos, offsets, -1.0), axis=1, keepdims=True)
        least = jnp.maximum(q_in + (half - WINDOW + 1), begin.astype(jnp.int32) + half - start)
        bias[b] = jnp.where((k_in >= least) & (k_in <= q_in + half), F32(0.0), F32(-1e30))

    row = lax.broadcasted_iota(jnp.int32, (rows, 1), 0)
    inner = row & (half - 1)
    source = (row - inner) + POOL * (inner & (mol_half - 1)) + (inner >> shift)
    col = lax.broadcasted_iota(jnp.int32, (rows, rows), 1)
    perm[...] = jnp.where(col == source, F32(1.0 / math.sqrt(HEAD_DIM)), F32(0.0)).astype(BF16)

    for name in ("slot", "st"):
        loads[name].wait()
    slot = slot_ref[0, 0]
    square = jnp.zeros((mol_rows, 1), F32)
    for c in range(chunks):
        cols = pl.ds(c * cw, cw)
        held = st_buf[slot, :, cols].astype(F32)
        square += jnp.sum(held * held, axis=1, keepdims=True)
    inv_rms = lax.rsqrt(square / width + EPS_NORM)
    pl.semaphore_wait(barrier, len(near))
    onward = [z_id(d)[1] for d in step_z] + [{"rep": lax.rem(rep + d, nrep)} for d in step_rep]
    signal(ready.at[0], onward)

    def remote(src, dst, send, recv, to):
        return pltpu.make_async_remote_copy(
            src_ref=src, dst_ref=dst, send_sem=send, recv_sem=recv, device_id=to, device_id_type=MESH
        )

    halo = []

    def send_halo(c):
        cols = pl.ds(c * cw, cw)
        for i, (src, dst) in enumerate(((k_hbm, k_buf), (v_hbm, v_buf))):
            copy = remote(
                src.at[0, 0, pl.ds(half, half), cols],
                dst.at[pl.ds(0, half), cols],
                kv_send.at[2 * c + i],
                kv_recv.at[2 * c + i],
                {"seq": seq_next},
            )
            copy.start()
            halo.append(copy)

    early = min(EARLY, chunks - 1)
    for c in range(early):
        send_halo(c)

    for name in ("cot", "gain"):
        loads[name].wait()
    cot = cot_buf[...]
    mixed = jnp.zeros((mol_rows, 1), F32)
    for c in range(chunks):
        cols = pl.ds(c * cw, cw)
        loads["w%d" % c].wait()
        back = lax.dot_general(cot, w_buf[cols, :], (((1,), (1,)), ((), ())), preferred_element_type=F32)
        whitened = st_buf[slot, :, cols].astype(F32) * inv_rms
        total = jnp.sum(back * whitened, axis=0, keepdims=True)
        for i in range(cw // part):
            g_own[c * (cw // part) + i] = total[:, i * part : (i + 1) * part]
        scaled = back * gain_ref[:, cols]
        bg_buf[:, cols] = scaled
        mixed += jnp.sum(scaled * whitened, axis=1, keepdims=True)

    if onward:
        pl.semaphore_wait(ready.at[0], len(onward))
    signal(ready.at[1], [z_id(d)[1] for d in step_z])

    phase1 = []
    for d in range(1, nown):
        other, to = owner_id(d)
        copy = remote(g_own.at[other], r1.at[d], p1_send.at[d], p1_recv.at[d], to)
        copy.start()
        phase1.append(copy)
    load("q", q_hbm.at[0, 0], q_raw)
    load("k", k_hbm.at[0, 0], k_buf.at[pl.ds(half, rows)])
    load("v", v_hbm.at[0, 0], v_buf.at[pl.ds(half, rows)])

    mixed = mixed / width
    for c in range(chunks):
        cols = pl.ds(c * cw, cw)
        whitened = st_buf[slot, :, cols].astype(F32) * inv_rms
        din[:, cols] = (inv_rms * (bg_buf[:, cols] - whitened * mixed)).astype(BF16)
    up_copy = remote(din, up_ref.at[0, 0], up_send.at[0], up_recv.at[0], {"section": sec_prev})
    up_copy.start()

    lane = lax.broadcasted_iota(jnp.int32, (rows, 128), 1)
    loads["q"].wait()
    for c in range(chunks):
        moved = jnp.dot(perm[...], q_raw[:, pl.ds(c * cw, cw)], preferred_element_type=F32)
        for i in range(pairs):
            cols = pl.ds(c * cw + i * 128, 128)
            piece = moved[:, i * 128 : (i + 1) * 128]
            first = jnp.where(lane < HEAD_DIM, piece, 0.0).astype(BF16)
            second = jnp.where(lane < HEAD_DIM, 0.0, piece).astype(BF16)
            for b in range(2):
                q_buf[b, pl.ds(0, half), cols] = first[b * half : (b + 1) * half]
                q_buf[b, pl.ds(half, half), cols] = second[b * half : (b + 1) * half]

    low = lax.broadcasted_iota(jnp.int32, (half, 128), 1) < HEAD_DIM
    fours = jnp.full((2 * half, 128), POOL, BF16)

    def one_pair(b, pair):
        cols = pl.ds(pl.multiple_of(pair * 128, 128), 128)
        keys = k_buf[pl.ds(b * half, 2 * half), cols]
        values = v_buf[pl.ds(b * half, 2 * half), cols]
        scores = lax.dot_general(q_buf[b, :, cols], keys, (((1,), (1,)), ((), ())), preferred_element_type=F32)
        blocked = bias[b]
        weights = []
        for h in range(2):
            s = scores[h * half : (h + 1) * half] + blocked
            top = jnp.max(s, axis=1, keepdims=True)
            weights.append(jnp.exp2((s - top) * LOG2E).astype(BF16))
        mixed_heads = jnp.dot(
            jnp.concatenate(weights, axis=0),
            jnp.concatenate([values, fours], axis=1),
            preferred_element_type=F32,
        )
        first, second = mixed_heads[:half], mixed_heads[half:]
        out = jnp.where(low, first[:, :128], second[:, :128]) / jnp.where(low, first[:, 128:], second[:, 128:])
        mean = out[:mol_half]
        for t in range(1, POOL):
            mean += out[t * mol_half : (t + 1) * mol_half]
        pooled[pl.ds(b * mol_half, mol_half), cols] = mean.astype(BF16)

    def attend(b, first_pair, count):
        unroll = min(UNROLL, count)

        def few_pairs(i, carry):
            for j in range(unroll):
                one_pair(b, first_pair + unroll * i + j)
            return carry

        lax.fori_loop(0, count // unroll, few_pairs, 0)

    relay = []

    def send_pooled(rows_at, cols):
        copy = remote(
            pooled.at[rows_at, cols],
            arrived.at[rows_at, cols],
            po_send.at[len(relay)],
            po_recv.at[len(relay)],
            {"section": sec_next},
        )
        copy.start()
        relay.append(copy)

    all_pairs = width // 128
    loads["k"].wait()
    loads["v"].wait()
    attend(1, 0, all_pairs // 2)

    for copy in phase1:
        copy.wait_recv()
    summed = g_own[me]
    for d in range(1, nown):
        summed += r1[d]
    r2[z] = summed
    if step_z:
        pl.semaphore_wait(ready.at[1], len(step_z))
    phase2 = []
    for d in range(1, nz):
        other, to = z_id(d)
        copy = remote(r2.at[z], r2.at[z], p2_send.at[d], p2_recv.at[d], to)
        copy.start()
        phase2.append(copy)
    for c in range(early, chunks):
        send_halo(c)

    attend(1, all_pairs // 2, all_pairs // 2)
    send_pooled(pl.ds(mol_half, mol_half), pl.ds(0, width))
    acc[...] = jnp.zeros_like(acc)
    square = jnp.zeros((mol_rows, 1), F32)

    def near_part(c):
        halo[2 * c].wait_recv()
        halo[2 * c + 1].wait_recv()
        attend(0, c * pairs, pairs)
        send_pooled(pl.ds(0, mol_half), pl.ds(c * cw, cw))

    def project(c, square):
        cols = pl.ds(c * cw, cw)
        relay[1 + c].wait_recv()
        got = arrived[:, cols].astype(F32)
        acc[...] += jnp.dot((got * gain_ref[:, cols]).astype(BF16), w_buf[cols, :], preferred_element_type=F32)
        return square + jnp.sum(got * got, axis=1, keepdims=True)

    before = min(BEFORE, chunks - 1)
    for c in range(before):
        near_part(c)

    for d in range(1, nz):
        other = lax.rem(z + nz - d, nz)
        remote(r2.at[z], r2.at[other], p2_send.at[d], p2_recv.at[d], {"seq": seq_next}).wait_recv()
    summed = r2[0]
    for i in range(1, nz):
        summed += r2[i]
    r3[me] = summed
    phase3 = []
    for d in range(1, nown):
        other, to = owner_id(d)
        copy = remote(r3.at[me], r3.at[me], p3_send.at[d], p3_recv.at[d], to)
        copy.start()
        phase3.append(copy)

    relay[0].wait_recv()
    done = 0
    for c in range(before, chunks):
        near_part(c)
        if done < c:
            square = project(done, square)
            done += 1
    while done < chunks - 1:
        square = project(done, square)
        done += 1

    for d in range(1, nown):
        other = lax.rem(me + nown - d, nown)
        remote(r3.at[me], r3.at[other], p3_send.at[d], p3_recv.at[d], {"seq": seq_next}).wait_recv()
    power = jnp.zeros((1, 1), F32)
    for i in range(nown):
        power += jnp.sum(r3[i] * r3[i], axis=1, keepdims=True)
    inv_step = 1.0 / jnp.sqrt(power / width + EPS_STEP)
    for i in range(nown):
        gu_ref[:, pl.ds(i * part, part)] = r3[i] * inv_step

    square = project(chunks - 1, square)
    mol_ref[0, 0] = (acc[...] * lax.rsqrt(square / width + EPS_NORM)).astype(BF16)
    for copy in (*halo, *phase1, *phase2, *phase3, *relay):
        copy.wait_send()
    up_copy.wait()


def write_out(*refs):
    count = (len(refs) - 1) // 2
    sem = refs[-1]
    copies = [pltpu.make_async_copy(refs[i], refs[count + i], sem.at[i]) for i in range(count)]
    for copy in copies:
        copy.start()
    for copy in copies:
        copy.wait()


def solution(mesh):
    nsec, nseq, nrep = (mesh.shape[a] for a in ("section", "seq", "rep"))

    def local(q, k, v, doc_starts, w, gain, stashed, cotangent, plan_slot):
        rows, width = q.shape[2:]
        key_width = w.shape[2]
        slots, mol_rows = stashed.shape[2:4]
        half = rows // 2
        chunks = CHUNKS if width >= 2048 else 2
        nz, nown = nseq // 2, nrep * 2
        part = width // nown
        hbm = pl.BlockSpec(memory_space=IN_SPACE)
        vmem = pl.BlockSpec(memory_space=pltpu.VMEM)
        dma = pltpu.SemaphoreType.DMA
        shapes = (
            ((1, 1, mol_rows, key_width), BF16),
            ((1, 1, mol_rows, width), BF16),
            ((1, width), F32),
        )
        results = pl.pallas_call(
            functools.partial(kernel, nsec, nseq, nrep, chunks),
            out_shape=tuple(OUT_SHAPE(s, t) for s, t in shapes),
            in_specs=[hbm] * 9,
            out_specs=(vmem, vmem, vmem),
            scratch_shapes=[
                pltpu.VMEM((rows, width), BF16),
                pltpu.VMEM((2, rows, width), BF16),
                pltpu.VMEM((rows + half, width), BF16),
                pltpu.VMEM((rows + half, width), BF16),
                pltpu.VMEM((width, key_width), BF16),
                pltpu.VMEM((slots, mol_rows, width), BF16),
                pltpu.VMEM((mol_rows, key_width), BF16),
                pltpu.VMEM((1, doc_starts.shape[2]), jnp.int32),
                pltpu.VMEM((1, width), F32),
                pltpu.SMEM((1, 1), jnp.int32),
                pltpu.VMEM((2, half, 2 * half), F32),
                pltpu.VMEM((mol_rows, width), F32),
                pltpu.VMEM((mol_rows, width), BF16),
                pltpu.VMEM((mol_rows, width), BF16),
                pltpu.VMEM((mol_rows, width), BF16),
                pltpu.VMEM((mol_rows, key_width), F32),
                pltpu.VMEM((rows, rows), BF16),
                pltpu.VMEM((nown, 1, part), F32),
                pltpu.VMEM((nown, 1, part), F32),
                pltpu.VMEM((nz, 1, part), F32),
                pltpu.VMEM((nown, 1, part), F32),
                dma((8 + chunks,)),
                pltpu.SemaphoreType.REGULAR((2,)),
                dma((2 * chunks,)),
                dma((2 * chunks,)),
                dma((1,)),
                dma((1,)),
                dma((chunks + 1,)),
                dma((chunks + 1,)),
                dma((nown,)),
                dma((nown,)),
                dma((nz,)),
                dma((nz,)),
                dma((nown,)),
                dma((nown,)),
            ],
            compiler_params=pltpu.CompilerParams(
                collective_id=0, has_side_effects=True, vmem_limit_bytes=56 * 1024 * 1024
            ),
        )(q, k, v, doc_starts, w, gain, stashed, cotangent, plan_slot)
        any_space = pl.BlockSpec(memory_space=pl.ANY)
        return pl.pallas_call(
            write_out,
            out_shape=tuple(jax.ShapeDtypeStruct(s, t) for s, t in shapes),
            in_specs=[vmem] * 3,
            out_specs=(any_space,) * 3,
            scratch_shapes=[dma((3,))],
        )(*(pltpu.with_memory_space_constraint(r, pltpu.VMEM) for r in results))

    in_specs = (
        P("rep", "section", "seq", None),
        P("rep", "section", "seq", None),
        P("rep", "section", "seq", None),
        P("rep", "section", None),
        P("section", None, None),
        P("section", None),
        P("rep", "section", None, "seq", None),
        P("rep", "section", "seq", None),
        P("rep", "section"),
    )
    out_specs = (
        P("rep", "section", "seq", None),
        P("rep", "section", "seq", None),
        P("section", None),
    )
    return jax.shard_map(local, mesh=mesh, in_specs=in_specs, out_specs=out_specs, check_vma=False)
```

```python
import functools
import math

import jax
import jax.numpy as jnp
from jax import lax
from jax.experimental import pallas as pl
from jax.experimental.pallas import tpu as pltpu
from jax.sharding import PartitionSpec as P

HEAD_DIM = 64
POOL = 4
WINDOW = 128
EPS_NORM = 1e-05
EPS_STEP = 1e-06
EARLY = 3
BEFORE = 3
CHUNKS = 4
UNROLL = 4
LOG2E = math.log2(math.e)
MESH = pl.DeviceIdType.MESH
F32 = jnp.float32
BF16 = jnp.bfloat16
IN_SPACE = pltpu.HBM
OUT_SHAPE = pltpu.VMEM


def kernel(
    nsec,
    nseq,
    nrep,
    chunks,
    q_hbm,
    k_hbm,
    v_hbm,
    doc_hbm,
    w_hbm,
    gain_hbm,
    st_hbm,
    cot_hbm,
    slot_hbm,
    mol_ref,
    up_ref,
    gu_ref,
    q_raw,
    q_buf,
    k_buf,
    v_buf,
    w_buf,
    st_buf,
    cot_buf,
    doc_ref,
    gain_ref,
    slot_ref,
    bias,
    bg_buf,
    din,
    pooled,
    arrived,
    acc,
    perm,
    g_own,
    r1,
    r2,
    r3,
    loc_sem,
    ready,
    kv_send,
    kv_recv,
    up_send,
    up_recv,
    po_send,
    po_recv,
    p1_send,
    p1_recv,
    p2_send,
    p2_recv,
    p3_send,
    p3_recv,
):
    rows, width = q_raw.shape
    half = rows // 2
    mol_rows, key_width = acc.shape
    mol_half = mol_rows // 2
    nz = nseq // 2
    nown = nrep * 2
    part = width // nown
    cw = width // chunks
    pairs = cw // 128

    sec = lax.axis_index("section")
    seq = lax.axis_index("seq")
    rep = lax.axis_index("rep")
    core = lax.rem(seq, 2)
    z = lax.div(seq, 2)
    me = rep * 2 + core
    sec_next = lax.rem(sec + 1, nsec)
    sec_prev = lax.rem(sec + nsec - 1, nsec)
    seq_next = lax.rem(seq + 1, nseq)
    across = lax.rem(seq + nseq + 2 * core - 1, nseq)

    def owner_id(d):
        other = lax.rem(me + d, nown)
        return other, {"seq": z * 2 + lax.rem(other, 2), "rep": lax.div(other, 2)}

    def z_id(d):
        other = lax.rem(z + d, nz)
        return other, {"seq": other * 2 + core}

    def signal(sem, peers):
        for peer in peers:
            pl.semaphore_signal(sem, inc=1, device_id=peer, device_id_type=MESH)

    near_z = sorted({d % nz for d in (1, 2, -1, -2)} - {0})
    step_z = sorted({2 % nz, -2 % nz} - {0})
    near = [{"seq": across}, {"section": sec_next}, {"section": sec_prev}]
    step_rep = sorted({1 % nrep, -1 % nrep} - {0})
    for d in [0] + step_rep:
        for e in range(2):
            if d or e:
                near.append({"seq": z * 2 + lax.rem(core + e, 2), "rep": lax.rem(rep + d, nrep)})
    near += [z_id(d)[1] for d in near_z]
    barrier = pltpu.get_barrier_semaphore()
    signal(barrier, near)

    loads = {}

    def load(name, src, dst):
        loads[name] = pltpu.make_async_copy(src, dst, loc_sem.at[len(loads)])
        loads[name].start()

    load("doc", doc_hbm.at[0], doc_ref)
    load("slot", slot_hbm, slot_ref)
    load("st", st_hbm.at[0, 0], st_buf)
    load("cot", cot_hbm.at[0, 0], cot_buf)
    load("gain", gain_hbm, gain_ref)
    for c in range(chunks):
        load("w%d" % c, w_hbm.at[0, pl.ds(c * cw, cw)], w_buf.at[pl.ds(c * cw, cw)])

    loads["doc"].wait()
    offsets = doc_ref[...].astype(F32)
    q_row = lax.broadcasted_iota(jnp.int32, (half, 1), 0)
    shift = mol_half.bit_length() - 1
    q_in = POOL * (q_row & (mol_half - 1)) + (q_row >> shift)
    k_in = lax.broadcasted_iota(jnp.int32, (half, 2 * half), 1)
    for b in range(2):
        start = seq * rows + b * half
        q_pos = (q_in + start).astype(F32)
        begin = jnp.max(jnp.where(offsets <= q_pos, offsets, -1.0), axis=1, keepdims=True)
        least = jnp.maximum(q_in + (half - WINDOW + 1), begin.astype(jnp.int32) + half - start)
        bias[b] = jnp.where((k_in >= least) & (k_in <= q_in + half), F32(0.0), F32(-1e30))

    row = lax.broadcasted_iota(jnp.int32, (rows, 1), 0)
    inner = row & (half - 1)
    source = (row - inner) + POOL * (inner & (mol_half - 1)) + (inner >> shift)
    col = lax.broadcasted_iota(jnp.int32, (rows, rows), 1)
    perm[...] = jnp.where(col == source, F32(1.0 / math.sqrt(HEAD_DIM)), F32(0.0)).astype(BF16)

    for name in ("slot", "st"):
        loads[name].wait()
    slot = slot_ref[0, 0]
    square = jnp.zeros((mol_rows, 1), F32)
    for c in range(chunks):
        cols = pl.ds(c * cw, cw)
        held = st_buf[slot, :, cols].astype(F32)
        square += jnp.sum(held * held, axis=1, keepdims=True)
    inv_rms = lax.rsqrt(square / width + EPS_NORM)
    pl.semaphore_wait(barrier, len(near))
    onward = [z_id(d)[1] for d in step_z] + [{"rep": lax.rem(rep + d, nrep)} for d in step_rep]
    signal(ready.at[0], onward)

    def remote(src, dst, send, recv, to):
        return pltpu.make_async_remote_copy(
            src_ref=src, dst_ref=dst, send_sem=send, recv_sem=recv, device_id=to, device_id_type=MESH
        )

    halo = []

    def send_halo(c):
        cols = pl.ds(c * cw, cw)
        for i, (src, dst) in enumerate(((k_hbm, k_buf), (v_hbm, v_buf))):
            copy = remote(
                src.at[0, 0, pl.ds(half, half), cols],
                dst.at[pl.ds(0, half), cols],
                kv_send.at[2 * c + i],
                kv_recv.at[2 * c + i],
                {"seq": seq_next},
            )
            copy.start()
            halo.append(copy)

    early = min(EARLY, chunks - 1)
    for c in range(early):
        send_halo(c)

    for name in ("cot", "gain"):
        loads[name].wait()
    cot = cot_buf[...]
    mixed = jnp.zeros((mol_rows, 1), F32)
    for c in range(chunks):
        cols = pl.ds(c * cw, cw)
        loads["w%d" % c].wait()
        back = lax.dot_general(cot, w_buf[cols, :], (((1,), (1,)), ((), ())), preferred_element_type=F32)
        whitened = st_buf[slot, :, cols].astype(F32) * inv_rms
        total = jnp.sum(back * whitened, axis=0, keepdims=True)
        for i in range(cw // part):
            g_own[c * (cw // part) + i] = total[:, i * part : (i + 1) * part]
        scaled = back * gain_ref[:, cols]
        bg_buf[:, cols] = scaled
        mixed += jnp.sum(scaled * whitened, axis=1, keepdims=True)

    if onward:
        pl.semaphore_wait(ready.at[0], len(onward))
    signal(ready.at[1], [z_id(d)[1] for d in step_z])

    phase1 = []
    for d in range(1, nown):
        other, to = owner_id(d)
        copy = remote(g_own.at[other], r1.at[d], p1_send.at[d], p1_recv.at[d], to)
        copy.start()
        phase1.append(copy)
    load("q", q_hbm.at[0, 0], q_raw)
    load("k", k_hbm.at[0, 0], k_buf.at[pl.ds(half, rows)])
    load("v", v_hbm.at[0, 0], v_buf.at[pl.ds(half, rows)])

    mixed = mixed / width
    for c in range(chunks):
        cols = pl.ds(c * cw, cw)
        whitened = st_buf[slot, :, cols].astype(F32) * inv_rms
        din[:, cols] = (inv_rms * (bg_buf[:, cols] - whitened * mixed)).astype(BF16)
    up_copy = remote(din, up_ref.at[0, 0], up_send.at[0], up_recv.at[0], {"section": sec_prev})
    up_copy.start()

    lane = lax.broadcasted_iota(jnp.int32, (rows, 128), 1)
    loads["q"].wait()
    for c in range(chunks):
        moved = jnp.dot(perm[...], q_raw[:, pl.ds(c * cw, cw)], preferred_element_type=F32)
        for i in range(pairs):
            cols = pl.ds(c * cw + i * 128, 128)
            piece = moved[:, i * 128 : (i + 1) * 128]
            first = jnp.where(lane < HEAD_DIM, piece, 0.0).astype(BF16)
            second = jnp.where(lane < HEAD_DIM, 0.0, piece).astype(BF16)
            for b in range(2):
                q_buf[b, pl.ds(0, half), cols] = first[b * half : (b + 1) * half]
                q_buf[b, pl.ds(half, half), cols] = second[b * half : (b + 1) * half]

    low = lax.broadcasted_iota(jnp.int32, (half, 128), 1) < HEAD_DIM
    fours = jnp.full((2 * half, 128), POOL, BF16)

    def one_pair(b, pair):
        cols = pl.ds(pl.multiple_of(pair * 128, 128), 128)
        keys = k_buf[pl.ds(b * half, 2 * half), cols]
        values = v_buf[pl.ds(b * half, 2 * half), cols]
        scores = lax.dot_general(q_buf[b, :, cols], keys, (((1,), (1,)), ((), ())), preferred_element_type=F32)
        blocked = bias[b]
        weights = []
        for h in range(2):
            s = scores[h * half : (h + 1) * half] + blocked
            top = jnp.max(s, axis=1, keepdims=True)
            weights.append(jnp.exp2((s - top) * LOG2E).astype(BF16))
        mixed_heads = jnp.dot(
            jnp.concatenate(weights, axis=0),
            jnp.concatenate([values, fours], axis=1),
            preferred_element_type=F32,
        )
        first, second = mixed_heads[:half], mixed_heads[half:]
        out = jnp.where(low, first[:, :128], second[:, :128]) / jnp.where(low, first[:, 128:], second[:, 128:])
        mean = out[:mol_half]
        for t in range(1, POOL):
            mean += out[t * mol_half : (t + 1) * mol_half]
        pooled[pl.ds(b * mol_half, mol_half), cols] = mean.astype(BF16)

    def attend(b, first_pair, count):
        unroll = min(UNROLL, count)

        def few_pairs(i, carry):
            for j in range(unroll):
                one_pair(b, first_pair + unroll * i + j)
            return carry

        lax.fori_loop(0, count // unroll, few_pairs, 0)

    relay = []

    def send_pooled(rows_at, cols):
        copy = remote(
            pooled.at[rows_at, cols],
            arrived.at[rows_at, cols],
            po_send.at[len(relay)],
            po_recv.at[len(relay)],
            {"section": sec_next},
        )
        copy.start()
        relay.append(copy)

    all_pairs = width // 128
    loads["k"].wait()
    loads["v"].wait()
    attend(1, 0, all_pairs // 2)
    send_pooled(pl.ds(mol_half, mol_half), pl.ds(0, width // 2))

    for copy in phase1:
        copy.wait_recv()
    summed = g_own[me]
    for d in range(1, nown):
        summed += r1[d]
    r2[z] = summed
    if step_z:
        pl.semaphore_wait(ready.at[1], len(step_z))
    phase2 = []
    for d in range(1, nz):
        other, to = z_id(d)
        copy = remote(r2.at[z], r2.at[z], p2_send.at[d], p2_recv.at[d], to)
        copy.start()
        phase2.append(copy)
    for c in range(early, chunks):
        send_halo(c)

    attend(1, all_pairs // 2, all_pairs // 2)
    send_pooled(pl.ds(mol_half, mol_half), pl.ds(width // 2, width // 2))
    acc[...] = jnp.zeros_like(acc)
    square = jnp.zeros((mol_rows, 1), F32)

    def near_part(c):
        halo[2 * c].wait_recv()
        halo[2 * c + 1].wait_recv()
        attend(0, c * pairs, pairs)
        send_pooled(pl.ds(0, mol_half), pl.ds(c * cw, cw))

    def project(c, square):
        cols = pl.ds(c * cw, cw)
        relay[2 + c].wait_recv()
        got = arrived[:, cols].astype(F32)
        acc[...] += jnp.dot((got * gain_ref[:, cols]).astype(BF16), w_buf[cols, :], preferred_element_type=F32)
        return square + jnp.sum(got * got, axis=1, keepdims=True)

    before = min(BEFORE, chunks - 1)
    for c in range(before):
        near_part(c)

    for d in range(1, nz):
        other = lax.rem(z + nz - d, nz)
        remote(r2.at[z], r2.at[other], p2_send.at[d], p2_recv.at[d], {"seq": seq_next}).wait_recv()
    summed = r2[0]
    for i in range(1, nz):
        summed += r2[i]
    r3[me] = summed
    phase3 = []
    for d in range(1, nown):
        other, to = owner_id(d)
        copy = remote(r3.at[me], r3.at[me], p3_send.at[d], p3_recv.at[d], to)
        copy.start()
        phase3.append(copy)

    relay[0].wait_recv()
    relay[1].wait_recv()
    done = 0
    for c in range(before, chunks):
        near_part(c)
        if done < c:
            square = project(done, square)
            done += 1
    while done < chunks - 1:
        square = project(done, square)
        done += 1

    for d in range(1, nown):
        other = lax.rem(me + nown - d, nown)
        remote(r3.at[me], r3.at[other], p3_send.at[d], p3_recv.at[d], {"seq": seq_next}).wait_recv()
    power = jnp.zeros((1, 1), F32)
    for i in range(nown):
        power += jnp.sum(r3[i] * r3[i], axis=1, keepdims=True)
    inv_step = 1.0 / jnp.sqrt(power / width + EPS_STEP)
    for i in range(nown):
        gu_ref[:, pl.ds(i * part, part)] = r3[i] * inv_step

    square = project(chunks - 1, square)
    mol_ref[0, 0] = (acc[...] * lax.rsqrt(square / width + EPS_NORM)).astype(BF16)
    for copy in (*halo, *phase1, *phase2, *phase3, *relay):
        copy.wait_send()
    up_copy.wait()


def write_out(*refs):
    count = (len(refs) - 1) // 2
    sem = refs[-1]
    copies = [pltpu.make_async_copy(refs[i], refs[count + i], sem.at[i]) for i in range(count)]
    for copy in copies:
        copy.start()
    for copy in copies:
        copy.wait()


def solution(mesh):
    nsec, nseq, nrep = (mesh.shape[a] for a in ("section", "seq", "rep"))

    def local(q, k, v, doc_starts, w, gain, stashed, cotangent, plan_slot):
        rows, width = q.shape[2:]
        key_width = w.shape[2]
        slots, mol_rows = stashed.shape[2:4]
        half = rows // 2
        chunks = CHUNKS if width >= 2048 else 2
        nz, nown = nseq // 2, nrep * 2
        part = width // nown
        hbm = pl.BlockSpec(memory_space=IN_SPACE)
        vmem = pl.BlockSpec(memory_space=pltpu.VMEM)
        dma = pltpu.SemaphoreType.DMA
        shapes = (
            ((1, 1, mol_rows, key_width), BF16),
            ((1, 1, mol_rows, width), BF16),
            ((1, width), F32),
        )
        results = pl.pallas_call(
            functools.partial(kernel, nsec, nseq, nrep, chunks),
            out_shape=tuple(OUT_SHAPE(s, t) for s, t in shapes),
            in_specs=[hbm] * 9,
            out_specs=(vmem, vmem, vmem),
            scratch_shapes=[
                pltpu.VMEM((rows, width), BF16),
                pltpu.VMEM((2, rows, width), BF16),
                pltpu.VMEM((rows + half, width), BF16),
                pltpu.VMEM((rows + half, width), BF16),
                pltpu.VMEM((width, key_width), BF16),
                pltpu.VMEM((slots, mol_rows, width), BF16),
                pltpu.VMEM((mol_rows, key_width), BF16),
                pltpu.VMEM((1, doc_starts.shape[2]), jnp.int32),
                pltpu.VMEM((1, width), F32),
                pltpu.SMEM((1, 1), jnp.int32),
                pltpu.VMEM((2, half, 2 * half), F32),
                pltpu.VMEM((mol_rows, width), F32),
                pltpu.VMEM((mol_rows, width), BF16),
                pltpu.VMEM((mol_rows, width), BF16),
                pltpu.VMEM((mol_rows, width), BF16),
                pltpu.VMEM((mol_rows, key_width), F32),
                pltpu.VMEM((rows, rows), BF16),
                pltpu.VMEM((nown, 1, part), F32),
                pltpu.VMEM((nown, 1, part), F32),
                pltpu.VMEM((nz, 1, part), F32),
                pltpu.VMEM((nown, 1, part), F32),
                dma((8 + chunks,)),
                pltpu.SemaphoreType.REGULAR((2,)),
                dma((2 * chunks,)),
                dma((2 * chunks,)),
                dma((1,)),
                dma((1,)),
                dma((chunks + 2,)),
                dma((chunks + 2,)),
                dma((nown,)),
                dma((nown,)),
                dma((nz,)),
                dma((nz,)),
                dma((nown,)),
                dma((nown,)),
            ],
            compiler_params=pltpu.CompilerParams(
                collective_id=0, has_side_effects=True, vmem_limit_bytes=56 * 1024 * 1024
            ),
        )(q, k, v, doc_starts, w, gain, stashed, cotangent, plan_slot)
        any_space = pl.BlockSpec(memory_space=pl.ANY)
        return pl.pallas_call(
            write_out,
            out_shape=tuple(jax.ShapeDtypeStruct(s, t) for s, t in shapes),
            in_specs=[vmem] * 3,
            out_specs=(any_space,) * 3,
            scratch_shapes=[dma((3,))],
        )(*(pltpu.with_memory_space_constraint(r, pltpu.VMEM) for r in results))

    in_specs = (
        P("rep", "section", "seq", None),
        P("rep", "section", "seq", None),
        P("rep", "section", "seq", None),
        P("rep", "section", None),
        P("section", None, None),
        P("section", None),
        P("rep", "section", None, "seq", None),
        P("rep", "section", "seq", None),
        P("rep", "section"),
    )
    out_specs = (
        P("rep", "section", "seq", None),
        P("rep", "section", "seq", None),
        P("section", None),
    )
    return jax.shard_map(local, mesh=mesh, in_specs=in_specs, out_specs=out_specs, check_vma=False)
```
